128 devices in a mesh: wide: 16 (over x_hi, z, core), narrow: 8 (over y, x_lo).
Axes of the slice: x: 4 (x_hi: 2, x_lo: 2; x = x_hi * 2 + x_lo), y: 4, z: 4, core: 2. Of those that a mesh axis runs over, the one named last changes fastest.
Arguments:
- block_states: bfloat16 [32, 64, 4096], P('wide', None, 'narrow'), may hold values from -6 to 6
- attn_gain: float32 [4096], replicated, may hold values from 0.1 to 1.9
- ffn_gain: float32 [4096], replicated, may hold values from 0.1 to 1.9
- final_gain: float32 [4096], replicated, may hold values from 0.1 to 1.9
- w_query: bfloat16 [4096, 4096], P(None, 'narrow'), may hold values from -0.09375 to 0.09375
- w_keyval: bfloat16 [4096, 1024], replicated, may hold values from -0.09375 to 0.09375
- w_out: bfloat16 [4096, 4096], P('narrow'), may hold values from -0.09375 to 0.09375
- w_gate: bfloat16 [4096, 1024], P(None, 'narrow'), may hold values from -0.09375 to 0.09375
- w_up: bfloat16 [4096, 1024], P(None, 'narrow'), may hold values from -0.09375 to 0.09375
- w_down: bfloat16 [1024, 4096], P('narrow'), may hold values from -0.1875 to 0.1875
- w_head: bfloat16 [4096, 131072], P(None, ('wide', 'narrow')), may hold values from -8 to 8
- cache: bfloat16 [32, 512, 4, 256], P('wide'), may hold values from -2000 to 2000
- prefix_lengths: int32 [32], P('wide'), may hold values from 128 to 512, as said below
- masked_positions: int32 [16, 64], replicated, may hold values from 0 to 63, as said below
Outputs:
- log_probs: float32 [1024, 131072], P(None, ('wide', 'narrow'))
- confidence: float32 [16, 64], replicated
The draws below stay inside these ranges and needn't reach their ends.
Inputs may be any that keep to these rules, and one draw needn't show every extreme that they name: `prefix_lengths`: some request branch has exactly 512 valid positions. `masked_positions`: the 64 positions of one request are distinct.
All inputs are finite; a program needn't handle non-finite values.
Results may differ from the reference program's by a relative error of at most 0.024.
The reference program's roundings to bfloat16 on the way count: a program that leaves them out, or rounds other values in their place, can miss the bound.
Values may be sent and summed in bfloat16 or wider, within the bound.
No kernel may reach another device: no remote copies, remote signals or barrier semaphores. Data moves between devices by JAX's collectives and lax.ppermute only.
A program may use at most 128 MiB of HBM per device.

```python
import math
import jax
import jax.numpy as jnp
from jax import lax

D = 4096
HEADS = 32
KVH = 4
HD = 128
SH = 1024
BLOCK = 64
PREFIX = 512
MASKED = 64
REQ = 16
V = 131072


def draw_w_head(key, part):
    key_base, key_scale = jax.random.split(jax.random.fold_in(key, 11), 2)
    base = jax.random.truncated_normal(key_base, -6.0, 6.0, (D, V), jnp.float32) * D ** (-0.5)
    col_scale = jnp.exp(jax.random.uniform(key_scale, (V,), jnp.float32, 0.0, jnp.log(10.0)))
    return jnp.clip(base * col_scale[None, :], -8.0, 8.0).astype(jnp.bfloat16)


def draw_cache(key, part):
    key_base = jax.random.fold_in(jax.random.fold_in(key, 23), 0)
    base = jax.random.truncated_normal(key_base, -6.0, 6.0, (2 * REQ, PREFIX, KVH, 2 * HD), jnp.float32)
    return base.astype(jnp.bfloat16)


def draw_prefix_lengths(key, part):
    key_len, key_which = jax.random.split(jax.random.fold_in(key, 37))
    lengths = jax.random.randint(key_len, (2 * REQ,), PREFIX // 4, PREFIX + 1)
    which = jax.random.randint(key_which, (), 0, 2 * REQ)
    return jnp.where(jnp.arange(2 * REQ) == which, PREFIX, lengths).astype(jnp.int32)


def draw_masked_positions(key, part):
    keys = jax.random.split(jax.random.fold_in(key, 41), REQ)
    chosen = jax.vmap(lambda single: jax.random.permutation(single, BLOCK)[:MASKED])(keys)
    return chosen.astype(jnp.int32)


def levels(own_key, shape, cuts, low, high):
    def one(position, shards_of):
        heights = jax.random.uniform(jax.random.fold_in(jax.random.fold_in(own_key, 6), position), (shards_of,), jnp.float32, low / len(cuts), high / len(cuts))
        return jnp.repeat(jnp.exp(heights), shape[position] // shards_of).reshape((-1,) + (1,) * (len(shape) - position - 1))

    factor_of = one(*cuts[0])
    for cut in cuts[1:]:
        factor_of = factor_of * one(*cut)
    return factor_of


def bell_draw(stream_key, extent, spread, reach, pieces=(), held_as=jnp.bfloat16):
    values = jax.random.normal(stream_key, extent, jnp.float32) * spread
    if len(pieces) > 0:
        values = levels(stream_key, extent, pieces, -0.22, 0.18) * values
    return jnp.clip(values, min=-reach, max=reach).astype(held_as)


def setup_inputs(seed: int = 0) -> dict:
    seeds = jax.random.split(jax.random.key(seed), 15)
    return {
        "block_states": bell_draw(seeds[0], (2 * REQ, BLOCK, D), 1.0, 6.0, ((0, 16), (2, 8))),
        "attn_gain": jnp.clip(1.0 + 0.18 * jax.random.normal(seeds[1], (D,), jnp.float32), 0.1, 1.9),
        "ffn_gain": jnp.clip(1.0 + 0.18 * jax.random.normal(seeds[2], (D,), jnp.float32), 0.1, 1.9),
        "final_gain": jnp.clip(1.0 + 0.18 * jax.random.normal(seeds[3], (D,), jnp.float32), 0.1, 1.9),
        "w_query": bell_draw(seeds[4], (D, HEADS * HD), D ** -0.5, 0.09375, ((1, 8),)),
        "w_keyval": bell_draw(seeds[5], (D, 2 * KVH * HD), D ** -0.5, 0.09375),
        "w_out": bell_draw(seeds[6], (HEADS * HD, D), (HEADS * HD) ** -0.5, 0.09375, ((0, 8),)),
        "w_gate": bell_draw(seeds[7], (D, SH), D ** -0.5, 0.09375, ((1, 8),)),
        "w_up": bell_draw(seeds[8], (D, SH), D ** -0.5, 0.09375, ((1, 8),)),
        "w_down": bell_draw(seeds[9], (SH, D), SH ** -0.5, 0.1875, ((0, 8),)),
        "w_head": draw_w_head(jax.random.fold_in(seeds[14], 71), 0),
        "cache": draw_cache(jax.random.fold_in(seeds[14], 71), 0),
        "prefix_lengths": draw_prefix_lengths(jax.random.fold_in(seeds[14], 71), 0),
        "masked_positions": draw_masked_positions(jax.random.fold_in(seeds[14], 71), 0),
    }


EPS = 1e-06
GUIDE = 1.5

def rms_scale(rows, gain):
    return rows * lax.rsqrt(lax.optimization_barrier(jnp.mean(rows * rows, axis=-1, keepdims=True)) + EPS) * gain

def attend_one(operands):
    query, cache_one, block_kv, length = operands
    group = HEADS // KVH
    query_four = query.astype(jnp.float32).reshape(MASKED, KVH, group, HD)
    scale = 1.0 / math.sqrt(HD)
    pre_keys = cache_one[:, :, :HD].astype(jnp.float32)
    pre_vals = cache_one[:, :, HD:].astype(jnp.float32)
    blk_keys = block_kv[:, :, 0, :].astype(jnp.float32)
    blk_vals = block_kv[:, :, 1, :].astype(jnp.float32)
    pre_scores = jnp.einsum('mkgd,pkd->kgmp', query_four, pre_keys) * scale
    live = jnp.arange(PREFIX) < length
    pre_scores = jnp.where(live, pre_scores, -jnp.inf)
    blk_scores = jnp.einsum('mkgd,pkd->kgmp', query_four, blk_keys) * scale
    scores = jnp.concatenate([pre_scores, blk_scores], axis=-1)
    peak = lax.optimization_barrier(jnp.max(scores, axis=-1, keepdims=True))
    weights = jnp.exp(scores - peak)
    probs = (weights / lax.optimization_barrier(jnp.sum(weights, axis=-1, keepdims=True))).astype(jnp.bfloat16)
    values = jnp.concatenate([pre_vals, blk_vals], axis=0)
    out = jnp.einsum('kgmp,pkd->mkgd', probs.astype(jnp.float32), values)
    return out.reshape(MASKED, HEADS * HD).astype(jnp.bfloat16)

def reference(block_states, attn_gain, ffn_gain, final_gain, w_query, w_keyval, w_out, w_gate, w_up, w_down, w_head, cache, prefix_lengths, masked_positions):
    states = block_states.astype(jnp.float32)
    normed = rms_scale(states, attn_gain).astype(jnp.bfloat16)
    keyval = jnp.einsum('bld,dc->blc', normed.astype(jnp.float32), w_keyval.astype(jnp.float32)).astype(jnp.bfloat16)
    keyval = keyval.reshape(2 * REQ, BLOCK, KVH, 2, HD)
    both_pos = jnp.concatenate([masked_positions, masked_positions], axis=0)
    picked = jax.vmap(lambda rows, idx: rows[idx])(block_states, both_pos)
    picked_normed = jax.vmap(lambda rows, idx: rows[idx])(normed, both_pos)
    query = jnp.einsum('bmd,dc->bmc', picked_normed.astype(jnp.float32), w_query.astype(jnp.float32)).astype(jnp.bfloat16)
    attended = lax.map(attend_one, (query, cache, keyval, prefix_lengths))
    first = picked.astype(jnp.float32) + jnp.einsum('bmc,cd->bmd', attended.astype(jnp.float32), w_out.astype(jnp.float32))
    ffn_in = rms_scale(first, ffn_gain).astype(jnp.bfloat16).astype(jnp.float32)
    gate_act = jnp.einsum('bmd,dc->bmc', ffn_in, w_gate.astype(jnp.float32))
    up_act = jnp.einsum('bmd,dc->bmc', ffn_in, w_up.astype(jnp.float32))
    hidden = (jax.nn.silu(gate_act) * up_act).astype(jnp.bfloat16)
    second = first + jnp.einsum('bmc,cd->bmd', hidden.astype(jnp.float32), w_down.astype(jnp.float32))
    final = rms_scale(second, final_gain)
    cond_rows = final[:REQ]
    uncond_rows = final[REQ:]
    guided = (uncond_rows + GUIDE * (cond_rows - uncond_rows)).astype(jnp.bfloat16).reshape(REQ * MASKED, D)
    logits = jnp.dot(guided, w_head, preferred_element_type=jnp.float32)
    peak = lax.optimization_barrier(jnp.max(logits, axis=-1))
    total = lax.optimization_barrier(jnp.sum(jnp.exp(logits - peak[:, None]), axis=-1))
    lse = peak + jnp.log(total)
    log_probs = logits - lse[:, None]
    confidence = jnp.exp(peak - lse).reshape(REQ, MASKED)
    return (log_probs, confidence)
```

```python
import math

import jax
import jax.numpy as jnp
from jax import lax
from jax.sharding import PartitionSpec as P

KVH = 4
HD = 128
EPS = 1e-06
GUIDE = 1.5
BOTH = ("wide", "narrow")


def flat(x, y, z, core):
    wide = (x // 2) * 8 + z * 2 + core
    narrow = y * 2 + x % 2
    return wide * 8 + narrow


def axis_groups(axis_of_core):
    groups = []
    for core in (0, 1):
        axis = axis_of_core[core]
        first, second = [name for name in "xyz" if name != axis]
        order = (0, 2, 1, 3) if axis == "x" else (0, 1, 2, 3)
        for i in range(4):
            for j in range(4):
                at = {first: i, second: j}
                groups.append(
                    [flat(**{**at, axis: step}, core=core) for step in order]
                )
    return groups


def rms_scale(rows, gain):
    return rows * lax.rsqrt(jnp.mean(rows * rows, axis=-1, keepdims=True) + EPS) * gain


def gather_narrow(rows):
    return lax.all_to_all(jnp.broadcast_to(rows[None], (8,) + rows.shape), "narrow", 0, 0)


def gather_groups(rows, groups):
    wide_rows = jnp.broadcast_to(rows[None], (4,) + rows.shape)
    return lax.all_to_all(wide_rows, BOTH, 0, 0, axis_index_groups=groups)


def scatter_sum(part):
    pieces = part.astype(jnp.bfloat16).reshape(8, part.shape[0] // 8, part.shape[1])
    received = lax.all_to_all(pieces, "narrow", 0, 0)
    return jnp.sum(received.astype(jnp.float32), axis=0)


def on_device(
    block_states,
    attn_gain,
    ffn_gain,
    final_gain,
    w_query,
    w_keyval,
    w_out,
    w_gate,
    w_up,
    w_down,
    w_head,
    cache,
    prefix_lengths,
    masked_positions,
):
    wide_index = lax.axis_index("wide")
    narrow_index = lax.axis_index("narrow")
    core = wide_index % 2
    is_upper = wide_index >= 8
    reqs, block, part_dim = block_states.shape
    rows = reqs * block
    dim = part_dim * 8

    first_req = wide_index % 8 * reqs
    my_positions = lax.dynamic_slice_in_dim(masked_positions, first_req, reqs, 0)
    choose = (my_positions[:, :, None] == jnp.arange(block)[None, None, :]).astype(jnp.bfloat16)
    picked_part = jnp.einsum(
        "bml,bld->bmd", choose, block_states, preferred_element_type=jnp.float32
    ).astype(jnp.bfloat16)
    full = gather_narrow(picked_part.reshape(rows, part_dim))
    full = jnp.transpose(full, (1, 0, 2)).reshape(rows, dim)
    normed = rms_scale(full.astype(jnp.float32), attn_gain).astype(jnp.bfloat16)

    kv_head = narrow_index // 2
    head_weight = lax.dynamic_slice_in_dim(w_keyval, kv_head * (2 * HD), 2 * HD, 1)
    block_kv = jnp.dot(normed, head_weight, preferred_element_type=jnp.float32)
    block_kv = block_kv.astype(jnp.bfloat16).reshape(reqs, block, 2 * HD)
    cache_kv = lax.dynamic_index_in_dim(cache, kv_head, axis=2, keepdims=False)
    local_heads = w_query.shape[1] // HD
    query = jnp.dot(normed, w_query, preferred_element_type=jnp.float32).astype(jnp.bfloat16)
    query = query.reshape(reqs, block, local_heads, HD)
    scale = 1.0 / math.sqrt(HD)
    pre_scores = (
        jnp.einsum("bmhd,bpd->bhmp", query, cache_kv[..., :HD], preferred_element_type=jnp.float32)
        * scale
    )
    live = jnp.arange(cache_kv.shape[1])[None, :] < prefix_lengths[:, None]
    pre_scores = jnp.where(live[:, None, None, :], pre_scores, -jnp.inf)
    blk_scores = (
        jnp.einsum("bmhd,bld->bhml", query, block_kv[..., :HD], preferred_element_type=jnp.float32)
        * scale
    )
    peak = jnp.maximum(
        jnp.max(pre_scores, axis=-1, keepdims=True), jnp.max(blk_scores, axis=-1, keepdims=True)
    )
    pre_weights = jnp.exp(pre_scores - peak)
    blk_weights = jnp.exp(blk_scores - peak)
    weight_total = jnp.sum(pre_weights, axis=-1, keepdims=True) + jnp.sum(
        blk_weights, axis=-1, keepdims=True
    )
    pre_probs = (pre_weights / weight_total).astype(jnp.bfloat16)
    blk_probs = (blk_weights / weight_total).astype(jnp.bfloat16)
    attended = jnp.einsum(
        "bhmp,bpd->bmhd", pre_probs, cache_kv[..., HD:], preferred_element_type=jnp.float32
    )
    attended = attended + jnp.einsum(
        "bhml,bld->bmhd", blk_probs, block_kv[..., HD:], preferred_element_type=jnp.float32
    )
    attended = attended.astype(jnp.bfloat16).reshape(rows, local_heads * HD)
    attn_part = jnp.dot(attended, w_out, preferred_element_type=jnp.float32)
    own_rows = rows // 8
    my_picked = lax.dynamic_slice_in_dim(full, narrow_index * own_rows, own_rows, 0)
    first = my_picked.astype(jnp.float32) + scatter_sum(attn_part)

    ffn_in = gather_narrow(rms_scale(first, ffn_gain).astype(jnp.bfloat16)).reshape(rows, dim)
    gate_act = jnp.dot(ffn_in, w_gate, preferred_element_type=jnp.float32)
    up_act = jnp.dot(ffn_in, w_up, preferred_element_type=jnp.float32)
    hidden = (jax.nn.silu(gate_act) * up_act).astype(jnp.bfloat16)
    ffn_part = jnp.dot(hidden, w_down, preferred_element_type=jnp.float32)
    final = rms_scale(first + scatter_sum(ffn_part), final_gain)

    half = own_rows // 2
    outgoing = jnp.where(is_upper, final[:half], final[half:])
    own_final = jnp.where(is_upper, final[half:], final[:half])
    partner = lax.ppermute(outgoing, "wide", [(i, i ^ 8) for i in range(16)])
    cond_rows = jnp.where(is_upper, partner, own_final)
    uncond_rows = jnp.where(is_upper, own_final, partner)
    guided = (uncond_rows + GUIDE * (cond_rows - uncond_rows)).astype(jnp.bfloat16)

    stage = gather_groups(guided, axis_groups("xx")).reshape(4 * half, dim)
    stage = gather_groups(stage, axis_groups("yz")).reshape(16 * half, dim)
    own_guided = gather_groups(stage, axis_groups("zy")).reshape(64 * half, dim)
    other_guided = lax.ppermute(own_guided, "wide", [(i, i ^ 1) for i in range(16)])

    def whole(own, other):
        zero = jnp.where(core == 0, own, other).reshape((4, 4, 4 * half) + own.shape[1:])
        one = jnp.where(core == 0, other, own).reshape((4, 4, 4 * half) + own.shape[1:])
        both = jnp.stack([zero, jnp.swapaxes(one, 0, 1)], axis=1)
        return both.reshape((128 * half,) + own.shape[1:])

    def head(rows_in):
        logits = jnp.dot(rows_in, w_head, preferred_element_type=jnp.float32)
        top = jnp.max(logits, axis=-1)
        return logits, top, jnp.sum(jnp.exp(logits - top[:, None]), axis=-1)

    own_logits, own_top, own_sum = head(own_guided)
    other_logits, other_top, other_sum = head(other_guided)
    stats = jnp.stack([whole(own_top, other_top), whole(own_sum, other_sum)])
    every = lax.all_to_all(jnp.broadcast_to(stats[None], (128,) + stats.shape), BOTH, 0, 0)
    row_peak = jnp.max(every[:, 0], axis=0)
    row_total = jnp.sum(every[:, 1] * jnp.exp(every[:, 0] - row_peak), axis=0)
    lse = row_peak + jnp.log(row_total)
    log_probs = whole(own_logits, other_logits) - lse[:, None]
    confidence = jnp.exp(row_peak - lse).reshape(-1, block)
    return (log_probs, confidence)


def solution(mesh):
    in_specs = (
        P("wide", None, "narrow"),
        P(),
        P(),
        P(),
        P(None, "narrow"),
        P(),
        P("narrow", None),
        P(None, "narrow"),
        P(None, "narrow"),
        P("narrow", None),
        P(None, ("wide", "narrow")),
        P("wide", None, None, None),
        P("wide"),
        P(),
    )
    out_specs = (P(None, ("wide", "narrow")), P())
    return jax.shard_map(
        on_device, mesh=mesh, in_specs=in_specs, out_specs=out_specs, check_vma=False
    )
```
